1024 devices in a mesh: ctx: 16 (over z_lo, core), tp: 64 (over y, z_hi, x).
Axes of the slice: x: 4, y: 8, z: 16 (z_hi: 2, z_lo: 8; z = z_hi * 8 + z_lo), core: 2. Of those that a mesh axis runs over, the one named last changes fastest.
Arguments:
- lin_query: bfloat16 [8192, 64, 128], P('ctx', 'tp'), may hold values from -6 to 6
- lin_key: bfloat16 [8192, 64, 128], P('ctx', 'tp'), may hold values from -6 to 6
- lin_value: bfloat16 [8192, 64, 128], P('ctx', 'tp'), may hold values from -6 to 6
- log_decay: float32 [64, 8192], P('tp', 'ctx'), may hold values from -2 to 0, as said below
- soft_query: bfloat16 [8192, 64, 128], P('ctx', 'tp'), may hold values from -12 to 12
- soft_key: bfloat16 [8192, 64, 128], P('ctx', 'tp'), may hold values from -4 to 4
- soft_value: bfloat16 [8192, 64, 128], P('ctx', 'tp'), may hold values from -6 to 6
Outputs:
- linear_out: bfloat16 [8192, 64, 128], P('ctx', 'tp')
- softmax_out: bfloat16 [8192, 64, 128], P('ctx', 'tp')
The draws below stay inside these ranges and needn't reach their ends.
Inputs may be any that keep to these rules, and one draw needn't show every extreme that they name: `log_decay`: every entry is negative.
All inputs are finite; a program needn't handle non-finite values.
Results may differ from the reference program's by a relative error of at most 0.0055.
Values may be sent and summed in bfloat16 or wider, within the bound.
A program may use at most 32 MiB of HBM per device.

```python
import math
import jax
import jax.numpy as jnp
from jax import lax

E = 128
TOK_DEV = 512
NUM_ATTN_GROUPS = 64
SEQUENCE_SPAN = 8192


def draw_log_decay(key, part):

    def sub(number):
        return jax.random.fold_in(key, number)
    fast = jax.random.bernoulli(sub(1), 0.5, (NUM_ATTN_GROUPS,))
    fast_rate = jax.random.uniform(sub(2), (NUM_ATTN_GROUPS,), jnp.float32, 1.0 / 50.0, 1.0 / 30.0)
    slow_rate = jax.random.uniform(sub(3), (NUM_ATTN_GROUPS,), jnp.float32, 0.02, 0.2) / SEQUENCE_SPAN
    base = jnp.where(fast, fast_rate, slow_rate)
    block_factor = jnp.exp(jax.random.uniform(sub(4), (NUM_ATTN_GROUPS, SEQUENCE_SPAN // TOK_DEV), jnp.float32, math.log(0.5), math.log(2.0)))
    token_factor = jnp.exp(jax.random.uniform(sub(5), (NUM_ATTN_GROUPS, SEQUENCE_SPAN), jnp.float32, math.log(1.0 / 3.0), math.log(3.0)))
    fading_speed = base[:, None] * jnp.repeat(block_factor, TOK_DEV, axis=1) * token_factor
    sequence_indices = jax.random.randint(sub(6), (NUM_ATTN_GROUPS, 3), 0, SEQUENCE_SPAN)
    fading_levels = jax.random.uniform(sub(7), (NUM_ATTN_GROUPS, 3), jnp.float32, math.log(0.6), math.log(0.8))
    sequence_segments = jnp.zeros((NUM_ATTN_GROUPS, SEQUENCE_SPAN), jnp.float32).at[jnp.arange(NUM_ATTN_GROUPS)[:, None], sequence_indices].add(fading_levels)
    return -fading_speed + sequence_segments


def query_key_pair(key):
    base_key = jax.random.fold_in(key, 4242)
    query = jnp.clip(jax.random.normal(jax.random.fold_in(base_key, 1), (SEQUENCE_SPAN, NUM_ATTN_GROUPS, E), jnp.float32), -4.0, 4.0)
    keys = jnp.clip(jax.random.normal(jax.random.fold_in(base_key, 2), (SEQUENCE_SPAN, NUM_ATTN_GROUPS, E), jnp.float32), -4.0, 4.0)
    return (query, keys)


def draw_soft_query(key, part):
    return query_key_pair(key)[0].astype(jnp.bfloat16)


def draw_soft_key(key, part):
    return query_key_pair(key)[1].astype(jnp.bfloat16)


def shard_levels(key, dims, split, least, largest):
    factor_of = 1.0
    for dim, shards_of in split:
        heights = jax.random.uniform(jax.random.fold_in(jax.random.fold_in(key, 6), dim), (shards_of,), jnp.float32, least / len(split), largest / len(split))
        factor_of = factor_of * jnp.repeat(jnp.exp(heights), dims[dim] // shards_of).reshape((-1,) + (1,) * (len(dims) - 1 - dim))
    return factor_of


def gaussian(own_key, shape, scale, most, cuts=(), dtype=jnp.bfloat16):
    factor_of = shard_levels(own_key, shape, cuts, -0.22, 0.18) if cuts else 1.0
    array = jax.random.normal(own_key, shape, jnp.float32) * scale * factor_of
    return jnp.minimum(jnp.maximum(array, -most), most).astype(dtype)


def setup_inputs(seed: int = 0) -> dict:
    key_of = jax.random.split(jax.random.key(seed), 8)
    lin_query = gaussian(key_of[0], (SEQUENCE_SPAN, NUM_ATTN_GROUPS, E), 1.0, 6.0, ((0, 16), (1, 64)))
    lin_key = gaussian(key_of[1], (SEQUENCE_SPAN, NUM_ATTN_GROUPS, E), 1.0, 6.0, ((0, 16), (1, 64)))
    lin_value = gaussian(key_of[2], (SEQUENCE_SPAN, NUM_ATTN_GROUPS, E), 1.0, 6.0, ((0, 16), (1, 64)))
    log_decay = draw_log_decay(jax.random.fold_in(key_of[7], 71), 0)
    soft_query = draw_soft_query(jax.random.fold_in(key_of[7], 71), 0)
    soft_key = draw_soft_key(jax.random.fold_in(key_of[7], 71), 0)
    soft_value = gaussian(key_of[6], (SEQUENCE_SPAN, NUM_ATTN_GROUPS, E), 1.0, 6.0, ((0, 16), (1, 64)))
    return dict(lin_query=lin_query, lin_key=lin_key, lin_value=lin_value, log_decay=log_decay, soft_query=soft_query, soft_key=soft_key, soft_value=soft_value)


def lightning(lin_query, lin_key, lin_value, log_decay):
    blocks = SEQUENCE_SPAN // TOK_DEV
    heads = lin_query.shape[1]
    width = lin_query.shape[2]
    qb = lin_query.reshape(blocks, TOK_DEV, heads, width)
    kb = lin_key.reshape(blocks, TOK_DEV, heads, width)
    vb = lin_value.reshape(blocks, TOK_DEV, heads, width)
    lb = jnp.transpose(log_decay.reshape(heads, blocks, TOK_DEV), (1, 0, 2))
    lower = jnp.arange(TOK_DEV)[:, None] >= jnp.arange(TOK_DEV)[None, :]

    def advance(state, inputs):
        query, key, value, logs = inputs
        cum = jnp.cumsum(logs, axis=1)
        diff = cum[:, :, None] - cum[:, None, :]
        mask = jnp.exp(jnp.where(lower[None], diff, -1e+30))
        scores = jnp.einsum('thd,shd->hts', query.astype(jnp.float32), key.astype(jnp.float32))
        weights = (scores * mask).astype(jnp.bfloat16)
        intra = jnp.einsum('hts,she->the', weights.astype(jnp.float32), value.astype(jnp.float32))
        rounded = lax.optimization_barrier(state.astype(jnp.bfloat16))
        inter = jnp.einsum('thd,hde->the', query.astype(jnp.float32), rounded.astype(jnp.float32))
        inter = inter * jnp.exp(cum).T[:, :, None]
        raw = intra + inter
        normed = raw * lax.rsqrt(lax.optimization_barrier(jnp.mean(raw * raw, axis=-1, keepdims=True)) + 1e-06)
        last = cum[:, -1]
        decayed = (key.astype(jnp.float32) * jnp.exp(last[None, :] - cum.T)[:, :, None]).astype(jnp.bfloat16)
        local = jnp.einsum('thd,the->hde', decayed.astype(jnp.float32), value.astype(jnp.float32))
        new_state = jnp.exp(last)[:, None, None] * state + local
        return (new_state, normed.astype(jnp.bfloat16))
    start = jnp.zeros((heads, width, width), jnp.float32)
    final, outs = lax.scan(advance, start, (qb, kb, vb, lb))
    return outs.reshape(SEQUENCE_SPAN, heads, width)

def softmax_layer(soft_query, soft_key, soft_value):
    width = soft_query.shape[2]
    scale = 1.0 / jnp.sqrt(jnp.float32(width))
    blocks = SEQUENCE_SPAN // TOK_DEV
    key_pos = jnp.arange(SEQUENCE_SPAN)

    def one_head(inputs):
        query, key, value = inputs
        qb = query.reshape(blocks, TOK_DEV, width)

        def one_block(pair):
            index, rows = pair
            q_pos = index * TOK_DEV + jnp.arange(TOK_DEV)
            scores = jnp.dot(rows, key.T, preferred_element_type=jnp.float32) * scale
            mask = q_pos[:, None] >= key_pos[None, :]
            scores = jnp.where(mask, scores, -1e+30)
            top = lax.optimization_barrier(jnp.max(scores, axis=1, keepdims=True))
            probs = jnp.where(mask, jnp.exp(scores - top), 0.0)
            total = lax.optimization_barrier(jnp.sum(probs, axis=1, keepdims=True))
            summed = jnp.dot(probs.astype(jnp.bfloat16), value, preferred_element_type=jnp.float32)
            return (summed / total).astype(jnp.bfloat16)
        outs = lax.map(one_block, (jnp.arange(blocks), qb))
        return outs.reshape(SEQUENCE_SPAN, width)
    per_head = lax.map(one_head, (jnp.moveaxis(soft_query, 1, 0), jnp.moveaxis(soft_key, 1, 0), jnp.moveaxis(soft_value, 1, 0)))
    return jnp.moveaxis(per_head, 0, 1)

def reference(lin_query, lin_key, lin_value, log_decay, soft_query, soft_key, soft_value):
    linear_out = lightning(lin_query, lin_key, lin_value, log_decay)
    softmax_out = softmax_layer(soft_query, soft_key, soft_value)
    return (linear_out, softmax_out)
```

```python
import functools
import math

import jax
import jax.numpy as jnp
from jax import lax
from jax.experimental import pallas as pl
from jax.experimental.pallas import tpu as pltpu
from jax.sharding import PartitionSpec as P

MESH = pl.DeviceIdType.MESH
ROWS = 512
E = 128
CHIPS = 8
TILE = 128
RELAY = 2
SCALE = 1.0 / math.sqrt(E)
NEG = -1e30
WRAP = True


def dot_nt(a, b):
    return lax.dot_general(a, b, (((1,), (1,)), ((), ())), preferred_element_type=jnp.float32)


def dot_tn(a, b):
    return lax.dot_general(a, b, (((0,), (0,)), ((), ())), preferred_element_type=jnp.float32)


def dot_nn(a, b):
    return jnp.dot(a, b, preferred_element_type=jnp.float32)


def kernel(
    lq, lk, lv, ld, sq, sk, sv,
    lin_out, soft_out,
    kv, relay, top, total, summed, intra, cumcol, state, sib_state, carry, onward,
    own_sem, up_send, z_recv, sib_send, sib_recv, ring_send, ring_recv, x_send, x_recv,
    c_send, c_recv,
):
    me = lax.axis_index("ctx")
    tp = lax.axis_index("tp")
    k = me // 2
    c = me % 2
    sib = me + 1 - 2 * c
    other = tp + 4 - 8 * ((tp // 4) % 2)

    def first_up(chip):
        return jnp.maximum(chip - 5, 0) if WRAP else 0 * chip

    def to(ctx, group=None):
        return {"ctx": ctx} if group is None else {"ctx": ctx, "tp": group}

    barrier = pltpu.get_barrier_semaphore()

    def greet(device):
        pl.semaphore_signal(barrier, inc=1, device_id=device, device_id_type=MESH)

    greet(to(sib))

    @pl.when(k < CHIPS - 1)
    def _():
        greet(to(me + 2))

    @pl.when(k > 0)
    def _():
        greet(to(me - 2))

    expected = 1 + jnp.where(k < CHIPS - 1, 1, 0) + jnp.where(k > 0, 1, 0)
    if WRAP:
        @pl.when(k < 2)
        def _():
            greet(to(2 * RELAY + c, other))

        @pl.when(k == CHIPS - 1)
        def _():
            greet(to(2 * RELAY + c, other))

        @pl.when(k == RELAY)
        def _():
            greet(to(c, other))
            greet(to(2 + c, other))
            greet(to(2 * CHIPS - 2 + c, other))

        expected = expected + jnp.where(k < 2, 1, 0) + jnp.where(k == CHIPS - 1, 1, 0)
        expected = expected + jnp.where(k == RELAY, 3, 0)
    pl.semaphore_wait(barrier, expected)

    def remote(src, dst, send, recv, device):
        return pltpu.make_async_remote_copy(
            src_ref=src, dst_ref=dst, send_sem=send, recv_sem=recv,
            device_id=device, device_id_type=MESH,
        )

    def up_copy(src, b, t):
        return remote(src, kv.at[2 * b + c, t], up_send.at[b, t], z_recv.at[b, t], to(me + 2))

    def down_copy(src, b, t):
        return remote(src, kv.at[2 * b + c, t], up_send.at[b, t], z_recv.at[b, t], to(me - 2))

    def sib_copy(src, b, t):
        return remote(src, kv.at[2 * b + c, t], sib_send.at[b, t], sib_recv.at[b, t], to(sib))

    def ring_copy(src, t):
        return remote(
            src, relay.at[k, t], ring_send.at[0, t], ring_recv.at[k, t],
            to(2 * RELAY + c, other),
        )

    def relay_copy(b, t):
        return remote(
            relay.at[b, t], kv.at[2 * b + c, t], ring_send.at[b, t], z_recv.at[b, t],
            to(2 * CHIPS - 2 + c, other),
        )

    own = (sk, sv)
    for t in range(2):
        @pl.when(k < CHIPS - 1)
        def _(t=t):
            up_copy(own[t], k, t).start()

        if WRAP:
            @pl.when(k < 2)
            def _(t=t):
                ring_copy(own[t], t).start()

        @pl.when(c == 0)
        def _(t=t):
            sib_copy(own[t], k, t).start()

    for t in range(2):
        pltpu.make_async_copy(own[t], kv.at[me, t], own_sem.at[t]).start()

    cum = jnp.broadcast_to(ld[...], (8, ROWS))
    lane = lax.broadcasted_iota(jnp.int32, (8, ROWS), 1)
    shift = 1
    while shift < ROWS:
        cum = cum + jnp.where(lane >= shift, pltpu.roll(cum, shift, 1), 0.0)
        shift *= 2
    row = cum[0:1]
    cumcol[...] = jnp.transpose(jnp.broadcast_to(row, (E, ROWS)))
    last = cumcol[ROWS - 1:ROWS, :]
    decayed = (lk[...].astype(jnp.float32) * jnp.exp(last - cumcol[...])).astype(jnp.bfloat16)
    state[0:E, :] = dot_tn(decayed, lv[...])
    state[E:E + 8, :] = jnp.broadcast_to(jnp.exp(last), (8, E))
    exchange = remote(state, sib_state, x_send, x_recv, to(sib))
    exchange.start()

    lower = (
        lax.broadcasted_iota(jnp.int32, (TILE, TILE), 0)
        >= lax.broadcasted_iota(jnp.int32, (TILE, TILE), 1)
    )
    for r in range(ROWS // TILE):
        mine = slice(r * TILE, (r + 1) * TILE)
        part = jnp.zeros((TILE, E), jnp.float32)
        for s in range(r + 1):
            theirs = slice(s * TILE, (s + 1) * TILE)
            diff = cumcol[mine, :] - row[:, theirs]
            if s == r:
                diff = jnp.where(lower, diff, NEG)
            weight = (dot_nt(lq[mine, :], lk[theirs, :]) * jnp.exp(diff)).astype(jnp.bfloat16)
            part = part + dot_nn(weight, lv[theirs, :])
        intra[mine, :] = part

    for t in range(2):
        pltpu.make_async_copy(own[t], kv.at[me, t], own_sem.at[t]).wait()
    for r in range(ROWS // TILE):
        mine = slice(r * TILE, (r + 1) * TILE)
        reach = (r + 1) * TILE
        score = dot_nt(sq[mine, :], kv[me, 0, 0:reach, :]) * SCALE
        allowed = (
            lax.broadcasted_iota(jnp.int32, (TILE, reach), 0) + r * TILE
            >= lax.broadcasted_iota(jnp.int32, (TILE, reach), 1)
        )
        score = jnp.where(allowed, score, NEG)
        peak = jnp.broadcast_to(jnp.max(score, axis=1, keepdims=True), (TILE, E))
        prob = jnp.exp(score - jnp.concatenate([peak] * (r + 1), axis=1))
        top[mine, :] = peak
        total[mine, :] = jnp.broadcast_to(jnp.sum(prob, axis=1, keepdims=True), (TILE, E))
        summed[mine, :] = dot_nn(prob.astype(jnp.bfloat16), kv[me, 1, 0:reach, :])

    def update(slot):
        keys = kv[slot, 0]
        values = kv[slot, 1]
        for r in range(ROWS // TILE):
            mine = slice(r * TILE, (r + 1) * TILE)
            score = dot_nt(sq[mine, :], keys) * SCALE
            before = top[mine, :]
            peak = jnp.maximum(before, jnp.max(score, axis=1, keepdims=True))
            prob = jnp.exp(score - jnp.concatenate([peak] * (ROWS // E), axis=1))
            fade = jnp.exp(before - peak)
            top[mine, :] = peak
            total[mine, :] = total[mine, :] * fade + jnp.sum(prob, axis=1, keepdims=True)
            summed[mine, :] = summed[mine, :] * fade + dot_nn(prob.astype(jnp.bfloat16), values)

    @pl.when(c == 1)
    def _():
        for t in range(2):
            sib_copy(kv.at[me - 1, t], k, t).wait_recv()
        update(me - 1)

    exchange.wait_recv()
    half = E // 2

    def up_carry():
        return remote(
            onward, carry.at[pl.ds(c * half, half)], c_send.at[0], c_recv.at[0], to(me + 2)
        )

    def side_carry():
        return remote(
            carry.at[pl.ds(c * half, half)], carry.at[pl.ds(c * half, half)],
            c_send.at[1], c_recv.at[1], to(sib),
        )

    def chip_state():
        even = jnp.where(c == 0, 1.0, 0.0)
        odd = 1.0 - even
        f_me = state[E:E + 1, :]
        f_sib = sib_state[E:E + 1, :]
        mine = state[pl.ds(c * half, half), :]
        theirs = sib_state[pl.ds(c * half, half), :]
        f_odd = f_me * odd + f_sib * even
        s_even = mine * even + theirs * odd
        s_odd = mine * odd + theirs * even
        return f_me * f_sib, f_odd * s_even + s_odd

    @pl.when(k == 0)
    def _():
        carry[...] = jnp.zeros((E, E), jnp.float32)
        onward[...] = chip_state()[1]
        up_carry().start()

    def pass_carry():
        up_carry().wait_recv()
        side_carry().start()

        @pl.when(k < CHIPS - 1)
        def _():
            factor, added = chip_state()
            onward[...] = factor * carry[pl.ds(c * half, half), :] + added
            up_carry().start()

    carry_step = (k + 2) // 2 + 3 * (k // 7)

    def sends_up(b):
        return (k < CHIPS - 1) & (b >= first_up(k + 1))

    def step(s, _):
        b = k - s
        if WRAP:
            b7 = jnp.where(s <= 3, 7 - s, jnp.where(s <= 5, s - 4, 9 - s))
            b6 = jnp.where(s <= 4, 6 - s, s - 5)
            b = jnp.where(k == 7, b7, jnp.where(k == 6, b6, b))
        for t in range(2):
            up_copy(kv.at[2 * b + c, t], b, t).wait_recv()

            @pl.when(sends_up(b))
            def _(t=t):
                up_copy(kv.at[2 * b + c, t], b, t).start()

            if WRAP:
                @pl.when((k == CHIPS - 1) & (b == 0))
                def _(t=t):
                    down_copy(kv.at[2 * b + c, t], b, t).start()

            sib_copy(kv.at[2 * b + c, t], b, t).start()
        update(2 * b + c)
        for t in range(2):
            sib_copy(kv.at[2 * b + 1 - c, t], b, t).wait_recv()
        update(2 * b + 1 - c)

        @pl.when(s == carry_step)
        def _():
            pass_carry()

        return 0

    lax.fori_loop(1, k + 1, step, 0)

    if WRAP:
        @pl.when(k == RELAY)
        def _():
            for b in range(2):
                for t in range(2):
                    ring_arrival = remote(
                        own[t], relay.at[b, t], ring_send.at[b, t], ring_recv.at[b, t], to(sib)
                    )
                    ring_arrival.wait_recv()
                    relay_copy(b, t).start()

    for r in range(ROWS // TILE):
        mine = slice(r * TILE, (r + 1) * TILE)
        soft_out[mine, :] = (summed[mine, :] / total[mine, :]).astype(soft_out.dtype)

    @pl.when(k > 0)
    def _():
        side_carry().wait_recv()

    even = jnp.where(c == 0, 1.0, 0.0)
    odd = 1.0 - even
    f_sib = sib_state[E:E + 1, :]
    entering = (
        carry[...] * (even + odd * f_sib) + odd * sib_state[0:E, :]
    ).astype(jnp.bfloat16)
    for r in range(ROWS // TILE):
        mine = slice(r * TILE, (r + 1) * TILE)
        raw = intra[mine, :] + dot_nn(lq[mine, :], entering) * jnp.exp(cumcol[mine, :])
        mean = jnp.mean(raw * raw, axis=1, keepdims=True)
        lin_out[mine, :] = (raw * lax.rsqrt(mean + 1e-06)).astype(lin_out.dtype)

    exchange.wait_send()

    @pl.when(k < CHIPS - 1)
    def _():
        up_carry().wait_send()

    @pl.when(k > 0)
    def _():
        side_carry().wait_send()

    def drain(b, _):
        for t in range(2):
            @pl.when(sends_up(b))
            def _(t=t):
                up_copy(kv.at[2 * b + c, t], b, t).wait_send()

            if WRAP:
                @pl.when((k == CHIPS - 1) & (b == 0))
                def _(t=t):
                    down_copy(kv.at[2 * b + c, t], b, t).wait_send()

            @pl.when((b < k) | (c == 0))
            def _(t=t):
                sib_copy(kv.at[2 * b + c, t], b, t).wait_send()
        return 0

    lax.fori_loop(0, k + 1, drain, 0)
    if WRAP:
        @pl.when(k < 2)
        def _():
            for t in range(2):
                ring_copy(own[t], t).wait_send()

        @pl.when(k == RELAY)
        def _():
            for b in range(2):
                for t in range(2):
                    relay_copy(b, t).wait_send()


def on_device(lin_query, lin_key, lin_value, log_decay, soft_query, soft_key, soft_value):
    def flat(array):
        return array.reshape(ROWS, E)

    vmem = pl.BlockSpec(memory_space=pltpu.VMEM)
    hbm = pl.BlockSpec(memory_space=pl.ANY)
    f32, bf16 = jnp.float32, jnp.bfloat16
    dma = pltpu.SemaphoreType.DMA
    lin, soft = pl.pallas_call(
        kernel,
        out_shape=[jax.ShapeDtypeStruct((ROWS, E), bf16)] * 2,
        in_specs=[vmem] * 5 + [hbm] * 2,
        out_specs=[vmem] * 2,
        scratch_shapes=[
            pltpu.VMEM((2 * CHIPS, 2, ROWS, E), bf16),
            pltpu.VMEM((2, 2, ROWS, E), bf16),
            pltpu.VMEM((ROWS, E), f32),
            pltpu.VMEM((ROWS, E), f32),
            pltpu.VMEM((ROWS, E), f32),
            pltpu.VMEM((ROWS, E), f32),
            pltpu.VMEM((ROWS, E), f32),
            pltpu.VMEM((E + 8, E), f32),
            pltpu.VMEM((E + 8, E), f32),
            pltpu.VMEM((E, E), f32),
            pltpu.VMEM((E // 2, E), f32),
            dma((2,)),
            dma((CHIPS, 2)),
            dma((CHIPS, 2)),
            dma((CHIPS, 2)),
            dma((CHIPS, 2)),
            dma((2, 2)),
            dma((2, 2)),
            dma,
            dma,
            dma((2,)),
            dma((2,)),
        ],
        compiler_params=pltpu.CompilerParams(collective_id=0, has_side_effects=True),
        name="hybrid_heads",
    )(
        flat(lin_query), flat(lin_key), flat(lin_value), log_decay,
        flat(soft_query), flat(soft_key), flat(soft_value),
    )
    return lin.reshape(ROWS, 1, E), soft.reshape(ROWS, 1, E)


def solution(mesh):
    wide = P("ctx", "tp", None)
    return jax.shard_map(
        on_device,
        mesh=mesh,
        in_specs=(wide, wide, wide, P("tp", "ctx"), wide, wide, wide),
        out_specs=(wide, wide),
        check_vma=False,
    )
```

```python
import functools
import math

import jax
import jax.numpy as jnp
from jax import lax
from jax.experimental import pallas as pl
from jax.experimental.pallas import tpu as pltpu
from jax.sharding import PartitionSpec as P

MESH = pl.DeviceIdType.MESH
ROWS = 512
E = 128
CHIPS = 8
TILE = 128
HELPER = 1
FIRST_HELPED = 5
HELPED = CHIPS - FIRST_HELPED
STAT = 16
SCALE = math.log2(math.e) / math.sqrt(E)
NEG = -1e30


def dot_nt(a, b):
    return lax.dot_general(a, b, (((1,), (1,)), ((), ())), preferred_element_type=jnp.float32)


def dot_tn(a, b):
    return lax.dot_general(a, b, (((0,), (0,)), ((), ())), preferred_element_type=jnp.float32)


def dot_nn(a, b):
    return jnp.dot(a, b, preferred_element_type=jnp.float32)


def kernel(
    lq_hbm, lk_hbm, lv_hbm, ld_hbm, sq_hbm, sk, sv,
    lin_out, soft_out,
    lq, lk, lv, ld, sq,
    kv, far_query, far_out, near_out, far_top, far_total, far_summed,
    top, total, summed, intra, cumcol, state, sib_state, carry, onward,
    own_sem, up_send, z_recv, sib_send, sib_recv, q_send, q_recv, o_send, o_recv, x_send, x_recv,
    c_send, c_recv,
):
    me = lax.axis_index("ctx")
    k = me // 2
    c = me % 2
    sib = me + 1 - 2 * c

    helped = k >= FIRST_HELPED

    def to(ctx):
        return {"ctx": ctx}

    barrier = pltpu.get_barrier_semaphore()

    def greet(device):
        pl.semaphore_signal(barrier, inc=1, device_id=device, device_id_type=MESH)

    greet(to(sib))

    @pl.when(k > 0)
    def _():
        greet(to(me - 2))

    @pl.when(k == HELPER)
    def _():
        for j in range(HELPED):
            greet(to(2 * (FIRST_HELPED + j) + c))

    local = [
        pltpu.make_async_copy(src, dst, own_sem.at[i])
        for i, (src, dst) in enumerate((
            (ld_hbm, ld), (lk_hbm, lk), (lv_hbm, lv), (lq_hbm, lq), (sq_hbm, sq),
            (sk, kv.at[me, 0]), (sv, kv.at[me, 1]),
        ))
    ]
    for copy in local:
        copy.start()

    expected = 1 + jnp.where(k < CHIPS - 1, 1, 0) + jnp.where(helped, 1, 0)
    pl.semaphore_wait(barrier, expected)

    def remote(src, dst, send, recv, device):
        return pltpu.make_async_remote_copy(
            src_ref=src, dst_ref=dst, send_sem=send, recv_sem=recv,
            device_id=device, device_id_type=MESH,
        )

    def up_copy(src, b, t):
        return remote(src, kv.at[2 * b + c, t], up_send.at[b, t], z_recv.at[b, t], to(me + 2))

    def sib_copy(src, b, t):
        return remote(src, kv.at[2 * b + c, t], sib_send.at[b, t], sib_recv.at[b, t], to(sib))

    def query_copy(j):
        return remote(sq_hbm, far_query.at[j], q_send, q_recv.at[j], to(2 * HELPER + c))

    def out_copy(j):
        return remote(
            far_out.at[j], near_out, o_send.at[j], o_recv, to(2 * (FIRST_HELPED + j) + c)
        )

    own = (sk, sv)

    own_to_sib = (c == 0) | (k == HELPER)

    def send_own(t):
        @pl.when(k < CHIPS - 1)
        def _():
            up_copy(own[t], k, t).start()

        @pl.when(own_to_sib)
        def _():
            sib_copy(own[t], k, t).start()

    send_own(0)

    @pl.when(helped)
    def _():
        query_copy(k - FIRST_HELPED).start()

    for copy in local[:3]:
        copy.wait()

    cum = jnp.broadcast_to(ld[...], (8, ROWS))
    lane = lax.broadcasted_iota(jnp.int32, (8, ROWS), 1)
    shift = 1
    while shift < ROWS:
        cum = cum + jnp.where(lane >= shift, pltpu.roll(cum, shift, 1), 0.0)
        shift *= 2
    row = cum[0:1]
    cumcol[...] = jnp.transpose(jnp.broadcast_to(row, (E, ROWS)))
    last = cumcol[ROWS - 1:ROWS, :]
    decayed = (lk[...].astype(jnp.float32) * jnp.exp(last - cumcol[...])).astype(jnp.bfloat16)
    state[0:E, :] = dot_tn(decayed, lv[...])
    state[E:E + 8, :] = jnp.broadcast_to(jnp.exp(last), (8, E))
    exchange = remote(state, sib_state, x_send, x_recv, to(sib))
    exchange.start()

    @pl.when(k > 0)
    def _():
        send_own(1)

    half = E // 2

    def up_carry():
        return remote(
            onward, carry.at[pl.ds(c * half, half)], c_send.at[0], c_recv.at[0], to(me + 2)
        )

    def side_carry():
        return remote(
            carry.at[pl.ds(c * half, half)], carry.at[pl.ds(c * half, half)],
            c_send.at[1], c_recv.at[1], to(sib),
        )

    def chip_state():
        even = jnp.where(c == 0, 1.0, 0.0)
        odd = 1.0 - even
        f_me = state[E:E + 1, :]
        f_sib = sib_state[E:E + 1, :]
        mine = state[pl.ds(c * half, half), :]
        theirs = sib_state[pl.ds(c * half, half), :]
        f_odd = f_me * odd + f_sib * even
        s_even = mine * even + theirs * odd
        s_odd = mine * odd + theirs * even
        return f_me * f_sib, f_odd * s_even + s_odd

    exchange.wait_recv()

    @pl.when(k == 0)
    def _():
        carry[...] = jnp.zeros((E, E), jnp.float32)
        onward[...] = chip_state()[1]
        up_carry().start()

    def pass_carry():
        up_carry().wait_recv()
        side_carry().start()

        @pl.when(k < CHIPS - 1)
        def _():
            factor, added = chip_state()
            onward[...] = factor * carry[pl.ds(c * half, half), :] + added
            up_carry().start()

    @pl.when(k == 0)
    def _():
        send_own(1)

    for copy in local[3:]:
        copy.wait()

    lower = (
        lax.broadcasted_iota(jnp.int32, (TILE, TILE), 0)
        >= lax.broadcasted_iota(jnp.int32, (TILE, TILE), 1)
    )
    for r in range(ROWS // TILE):
        mine = slice(r * TILE, (r + 1) * TILE)
        part = jnp.zeros((TILE, E), jnp.float32)
        for s in range(r + 1):
            theirs = slice(s * TILE, (s + 1) * TILE)
            diff = cumcol[mine, :] - row[:, theirs]
            if s == r:
                diff = jnp.where(lower, diff, NEG)
            weight = (dot_nt(lq[mine, :], lk[theirs, :]) * jnp.exp(diff)).astype(jnp.bfloat16)
            part = part + dot_nn(weight, lv[theirs, :])
        intra[mine, :] = part

    for r in range(ROWS // TILE):
        mine = slice(r * TILE, (r + 1) * TILE)
        reach = (r + 1) * TILE
        score = dot_nt(sq[mine, :], kv[me, 0, 0:reach, :]) * SCALE
        allowed = (
            lax.broadcasted_iota(jnp.int32, (TILE, reach), 0) + r * TILE
            >= lax.broadcasted_iota(jnp.int32, (TILE, reach), 1)
        )
        score = jnp.where(allowed, score, NEG)
        peak = jnp.broadcast_to(jnp.max(score, axis=1, keepdims=True), (TILE, E))
        prob = jnp.exp2(score - jnp.concatenate([peak] * (r + 1), axis=1))
        top[mine, :] = peak
        total[mine, :] = jnp.broadcast_to(jnp.sum(prob, axis=1, keepdims=True), (TILE, E))
        summed[mine, :] = dot_nn(prob.astype(jnp.bfloat16), kv[me, 1, 0:reach, :])

    def update(slot, query, top, total, summed):
        keys = kv[slot, 0]
        values = kv[slot, 1]
        for r in range(ROWS // TILE):
            mine = slice(r * TILE, (r + 1) * TILE)
            score = dot_nt(query[mine, :], keys) * SCALE
            before = top[mine, :]
            peak = jnp.maximum(before, jnp.max(score, axis=1, keepdims=True))
            prob = jnp.exp2(score - jnp.concatenate([peak] * (ROWS // E), axis=1))
            fade = jnp.exp2(before - peak)
            top[mine, :] = peak
            total[mine, :] = total[mine, :] * fade + jnp.sum(prob, axis=1, keepdims=True)
            summed[mine, :] = summed[mine, :] * fade + dot_nn(prob.astype(jnp.bfloat16), values)

    @pl.when(c == 1)
    def _():
        for t in range(2):
            sib_copy(kv.at[me - 1, t], k, t).wait_recv()
        update(me - 1, sq, top, total, summed)

    def sends_up(b):
        return (k < FIRST_HELPED - 1) | ((k < CHIPS - 1) & (b > HELPER))

    def step(s, _):
        b = k - s
        for t in range(2):
            up_copy(kv.at[2 * b + c, t], b, t).wait_recv()

            @pl.when(sends_up(b))
            def _(t=t):
                up_copy(kv.at[2 * b + c, t], b, t).start()

            sib_copy(kv.at[2 * b + c, t], b, t).start()
            if t == 0:
                @pl.when(b == 0)
                def _():
                    pass_carry()

        update(2 * b + c, sq, top, total, summed)
        for t in range(2):
            sib_copy(kv.at[2 * b + 1 - c, t], b, t).wait_recv()
        update(2 * b + 1 - c, sq, top, total, summed)
        return 0

    lax.fori_loop(1, jnp.where(helped, k - HELPER, k + 1), step, 0)

    @pl.when(helped)
    def _():
        pass_carry()

    tiles = [slice(r * TILE, (r + 1) * TILE) for r in range(ROWS // TILE)]

    @pl.when(k == HELPER)
    def _():
        for t in range(2):
            @pl.when(c == 0)
            def _(t=t):
                sib_copy(kv.at[me + 1, t], k, t).wait_recv()

        def one(i, _):
            j = HELPED - 1 - i
            query_copy(j).wait_recv()
            far_top[...] = jnp.full((ROWS, E), NEG, jnp.float32)
            far_total[...] = jnp.zeros((ROWS, E), jnp.float32)
            far_summed[...] = jnp.zeros((ROWS, E), jnp.float32)

            def over(u, _):
                update(2 * HELPER + 1 - u, far_query.at[j], far_top, far_total, far_summed)
                return 0

            lax.fori_loop(0, 2 * HELPER + 2, over, 0)
            stats = []
            for mine in tiles:
                far_out[j, mine, :] = (far_summed[mine, :] / far_total[mine, :]).astype(jnp.bfloat16)
                level = far_top[mine, :] + jnp.log2(far_total[mine, :])
                stats.append(jnp.transpose(level)[0:1, :])
            level = jnp.concatenate(stats, axis=0)
            high = level.astype(jnp.bfloat16).astype(jnp.float32)
            middle = (level - high).astype(jnp.bfloat16).astype(jnp.float32)
            low = level - high - middle
            far_out[j, ROWS:ROWS + STAT, :] = jnp.concatenate(
                [high, middle, low, jnp.zeros_like(low)], axis=0
            ).astype(jnp.bfloat16)
            out_copy(j).start()
            return 0

        lax.fori_loop(0, HELPED, one, 0)

    @pl.when(helped)
    def _():
        out_copy(0).wait_recv()
        parts = near_out[ROWS:ROWS + STAT, :].astype(jnp.float32)
        level = parts[0:4] + parts[4:8] + parts[8:12]
        for r, mine in enumerate(tiles):
            arrived = jnp.transpose(jnp.broadcast_to(level[r:r + 1, :], (TILE, E)))
            before = top[mine, :]
            peak = jnp.maximum(before, arrived)
            fade = jnp.exp2(before - peak)
            share = jnp.exp2(arrived - peak)
            total[mine, :] = total[mine, :] * fade + share
            summed[mine, :] = summed[mine, :] * fade + near_out[mine, :].astype(jnp.float32) * share

    for r in range(ROWS // TILE):
        mine = slice(r * TILE, (r + 1) * TILE)
        soft_out[mine, :] = (summed[mine, :] / total[mine, :]).astype(soft_out.dtype)

    @pl.when(k > 0)
    def _():
        side_carry().wait_recv()

    even = jnp.where(c == 0, 1.0, 0.0)
    odd = 1.0 - even
    f_sib = sib_state[E:E + 1, :]
    entering = (
        carry[...] * (even + odd * f_sib) + odd * sib_state[0:E, :]
    ).astype(jnp.bfloat16)
    for r in range(ROWS // TILE):
        mine = slice(r * TILE, (r + 1) * TILE)
        raw = intra[mine, :] + dot_nn(lq[mine, :], entering) * jnp.exp(cumcol[mine, :])
        mean = jnp.mean(raw * raw, axis=1, keepdims=True)
        lin_out[mine, :] = (raw * lax.rsqrt(mean + 1e-06)).astype(lin_out.dtype)

    exchange.wait_send()

    @pl.when(k < CHIPS - 1)
    def _():
        up_carry().wait_send()

    @pl.when(k > 0)
    def _():
        side_carry().wait_send()

    def drain(b, _):
        for t in range(2):
            @pl.when(sends_up(b))
            def _(t=t):
                up_copy(kv.at[2 * b + c, t], b, t).wait_send()

            @pl.when((b < k) | own_to_sib)
            def _(t=t):
                sib_copy(kv.at[2 * b + c, t], b, t).wait_send()
        return 0

    lax.fori_loop(jnp.where(helped, HELPER + 1, 0), k + 1, drain, 0)

    @pl.when(helped)
    def _():
        query_copy(0).wait_send()

    @pl.when(k == HELPER)
    def _():
        for j in range(HELPED):
            out_copy(j).wait_send()


def on_device(lin_query, lin_key, lin_value, log_decay, soft_query, soft_key, soft_value):
    def stay(array):
        return pltpu.with_memory_space_constraint(array, pltpu.MemorySpace.HBM)

    def flat(array):
        return stay(array.reshape(ROWS, E))

    vmem = pl.BlockSpec(memory_space=pltpu.VMEM)
    hbm = pl.BlockSpec(memory_space=pltpu.MemorySpace.HBM)
    f32, bf16 = jnp.float32, jnp.bfloat16
    dma = pltpu.SemaphoreType.DMA
    lin, soft = pl.pallas_call(
        kernel,
        out_shape=[jax.ShapeDtypeStruct((ROWS, E), bf16)] * 2,
        in_specs=[hbm] * 7,
        out_specs=[vmem] * 2,
        scratch_shapes=[
            pltpu.VMEM((ROWS, E), bf16),
            pltpu.VMEM((ROWS, E), bf16),
            pltpu.VMEM((ROWS, E), bf16),
            pltpu.VMEM((1, ROWS), f32),
            pltpu.VMEM((ROWS, E), bf16),
            pltpu.VMEM((2 * CHIPS, 2, ROWS, E), bf16),
            pltpu.VMEM((HELPED, ROWS, E), bf16),
            pltpu.VMEM((HELPED, ROWS + STAT, E), bf16),
            pltpu.VMEM((ROWS + STAT, E), bf16),
            pltpu.VMEM((ROWS, E), f32),
            pltpu.VMEM((ROWS, E), f32),
            pltpu.VMEM((ROWS, E), f32),
            pltpu.VMEM((ROWS, E), f32),
            pltpu.VMEM((ROWS, E), f32),
            pltpu.VMEM((ROWS, E), f32),
            pltpu.VMEM((ROWS, E), f32),
            pltpu.VMEM((ROWS, E), f32),
            pltpu.VMEM((E + 8, E), f32),
            pltpu.VMEM((E + 8, E), f32),
            pltpu.VMEM((E, E), f32),
            pltpu.VMEM((E // 2, E), f32),
            dma((7,)),
            dma((CHIPS, 2)),
            dma((CHIPS, 2)),
            dma((CHIPS, 2)),
            dma((CHIPS, 2)),
            dma,
            dma((HELPED,)),
            dma((HELPED,)),
            dma,
            dma,
            dma,
            dma((2,)),
            dma((2,)),
        ],
        compiler_params=pltpu.CompilerParams(
            collective_id=0, has_side_effects=True, vmem_limit_bytes=24 << 20
        ),
        name="hybrid_heads",
    )(
        flat(lin_query), flat(lin_key), flat(lin_value), stay(log_decay),
        flat(soft_query), flat(soft_key), flat(soft_value),
    )
    return lin.reshape(ROWS, 1, E), soft.reshape(ROWS, 1, E)


def solution(mesh):
    wide = P("ctx", "tp", None)
    return jax.shard_map(
        on_device,
        mesh=mesh,
        in_specs=(wide, wide, wide, P("tp", "ctx"), wide, wide, wide),
        out_specs=(wide, wide),
        check_vma=False,
    )
```

```python
import functools
import math

import jax
import jax.numpy as jnp
from jax import lax
from jax.experimental import pallas as pl
from jax.experimental.pallas import tpu as pltpu
from jax.sharding import PartitionSpec as P

MESH = pl.DeviceIdType.MESH
ROWS = 512
E = 128
CHIPS = 8
TILE = 128
HELPER = 1
FIRST_HELPED = 5
HELPED = CHIPS - FIRST_HELPED
STAT = 16
SCALE = math.log2(math.e) / math.sqrt(E)
NEG = -1e30


def dot_nt(a, b):
    return lax.dot_general(a, b, (((1,), (1,)), ((), ())), preferred_element_type=jnp.float32)


def dot_tn(a, b):
    return lax.dot_general(a, b, (((0,), (0,)), ((), ())), preferred_element_type=jnp.float32)


def dot_nn(a, b):
    return jnp.dot(a, b, preferred_element_type=jnp.float32)


def kernel(
    lq_hbm, lk_hbm, lv_hbm, ld_hbm, sq_hbm, sk, sv,
    lin_out, soft_out,
    lq, lk, lv, ld, sq,
    kv, far_query, far_out, near_out, far_top, far_total, far_summed,
    weights, fades, top, total, summed, intra, cumcol, state, sib_state, carry, onward,
    own_sem, up_send, z_recv, sib_send, sib_recv, q_send, q_recv, o_send, o_recv, x_send, x_recv,
    c_send, c_recv,
):
    me = lax.axis_index("ctx")
    k = me // 2
    c = me % 2
    sib = me + 1 - 2 * c

    helped = k >= FIRST_HELPED

    def to(ctx):
        return {"ctx": ctx}

    barrier = pltpu.get_barrier_semaphore()

    def greet(device):
        pl.semaphore_signal(barrier, inc=1, device_id=device, device_id_type=MESH)

    greet(to(sib))

    @pl.when(k > 0)
    def _():
        greet(to(me - 2))

    @pl.when(k == HELPER)
    def _():
        for j in range(HELPED):
            greet(to(2 * (FIRST_HELPED + j) + c))

    local = [
        pltpu.make_async_copy(src, dst, own_sem.at[i])
        for i, (src, dst) in enumerate((
            (ld_hbm, ld), (lk_hbm, lk), (lv_hbm, lv), (lq_hbm, lq), (sq_hbm, sq),
            (sk, kv.at[me, 0]), (sv, kv.at[me, 1]),
        ))
    ]
    for copy in local:
        copy.start()

    expected = 1 + jnp.where(k < CHIPS - 1, 1, 0) + jnp.where(helped, 1, 0)
    pl.semaphore_wait(barrier, expected)

    def remote(src, dst, send, recv, device):
        return pltpu.make_async_remote_copy(
            src_ref=src, dst_ref=dst, send_sem=send, recv_sem=recv,
            device_id=device, device_id_type=MESH,
        )

    def up_copy(src, b, t):
        return remote(src, kv.at[2 * b + c, t], up_send.at[b, t], z_recv.at[b, t], to(me + 2))

    def sib_copy(src, b, t):
        return remote(src, kv.at[2 * b + c, t], sib_send.at[b, t], sib_recv.at[b, t], to(sib))

    def query_copy(j):
        return remote(sq_hbm, far_query.at[j], q_send, q_recv.at[j], to(2 * HELPER + c))

    def out_copy(j):
        return remote(
            far_out.at[j], near_out, o_send.at[j], o_recv, to(2 * (FIRST_HELPED + j) + c)
        )

    own = (sk, sv)

    own_to_sib = (c == 0) | (k == HELPER)

    def send_own(t):
        @pl.when(k < CHIPS - 1)
        def _():
            up_copy(own[t], k, t).start()

        @pl.when(own_to_sib)
        def _():
            sib_copy(own[t], k, t).start()

    send_own(0)

    @pl.when(helped)
    def _():
        query_copy(k - FIRST_HELPED).start()

    for copy in local[:3]:
        copy.wait()

    cum = jnp.broadcast_to(ld[...], (8, ROWS))
    lane = lax.broadcasted_iota(jnp.int32, (8, ROWS), 1)
    shift = 1
    while shift < ROWS:
        cum = cum + jnp.where(lane >= shift, pltpu.roll(cum, shift, 1), 0.0)
        shift *= 2
    row = cum[0:1]
    cumcol[...] = jnp.transpose(jnp.broadcast_to(row, (E, ROWS)))
    last = cumcol[ROWS - 1:ROWS, :]
    decayed = (lk[...].astype(jnp.float32) * jnp.exp(last - cumcol[...])).astype(jnp.bfloat16)
    state[0:E, :] = dot_tn(decayed, lv[...])
    state[E:E + 8, :] = jnp.broadcast_to(jnp.exp(last), (8, E))
    exchange = remote(state, sib_state, x_send, x_recv, to(sib))
    exchange.start()

    @pl.when(k > 0)
    def _():
        send_own(1)

    half = E // 2

    def up_carry():
        return remote(
            onward, carry.at[pl.ds(c * half, half)], c_send.at[0], c_recv.at[0], to(me + 2)
        )

    def side_carry():
        return remote(
            carry.at[pl.ds(c * half, half)], carry.at[pl.ds(c * half, half)],
            c_send.at[1], c_recv.at[1], to(sib),
        )

    def chip_state():
        even = jnp.where(c == 0, 1.0, 0.0)
        odd = 1.0 - even
        f_me = state[E:E + 1, :]
        f_sib = sib_state[E:E + 1, :]
        mine = state[pl.ds(c * half, half), :]
        theirs = sib_state[pl.ds(c * half, half), :]
        f_odd = f_me * odd + f_sib * even
        s_even = mine * even + theirs * odd
        s_odd = mine * odd + theirs * even
        return f_me * f_sib, f_odd * s_even + s_odd

    exchange.wait_recv()

    @pl.when(k == 0)
    def _():
        carry[...] = jnp.zeros((E, E), jnp.float32)
        onward[...] = chip_state()[1]
        up_carry().start()

    def pass_carry():
        up_carry().wait_recv()
        side_carry().start()

        @pl.when(k < CHIPS - 1)
        def _():
            factor, added = chip_state()
            onward[...] = factor * carry[pl.ds(c * half, half), :] + added
            up_carry().start()

    @pl.when(k == 0)
    def _():
        send_own(1)

    for copy in local[3:]:
        copy.wait()

    lower = (
        lax.broadcasted_iota(jnp.int32, (TILE, TILE), 0)
        >= lax.broadcasted_iota(jnp.int32, (TILE, TILE), 1)
    )
    for r in range(ROWS // TILE):
        mine = slice(r * TILE, (r + 1) * TILE)
        part = jnp.zeros((TILE, E), jnp.float32)
        for s in range(r + 1):
            theirs = slice(s * TILE, (s + 1) * TILE)
            diff = cumcol[mine, :] - row[:, theirs]
            if s == r:
                diff = jnp.where(lower, diff, NEG)
            weight = (dot_nt(lq[mine, :], lk[theirs, :]) * jnp.exp(diff)).astype(jnp.bfloat16)
            part = part + dot_nn(weight, lv[theirs, :])
        intra[mine, :] = part

    for r in range(ROWS // TILE):
        mine = slice(r * TILE, (r + 1) * TILE)
        reach = (r + 1) * TILE
        score = dot_nt(sq[mine, :], kv[me, 0, 0:reach, :]) * SCALE
        allowed = (
            lax.broadcasted_iota(jnp.int32, (TILE, reach), 0) + r * TILE
            >= lax.broadcasted_iota(jnp.int32, (TILE, reach), 1)
        )
        score = jnp.where(allowed, score, NEG)
        peak = jnp.broadcast_to(jnp.max(score, axis=1, keepdims=True), (TILE, E))
        prob = jnp.exp2(score - jnp.concatenate([peak] * (r + 1), axis=1))
        top[mine, :] = peak
        total[mine, :] = jnp.broadcast_to(jnp.sum(prob, axis=1, keepdims=True), (TILE, E))
        summed[mine, :] = dot_nn(prob.astype(jnp.bfloat16), kv[me, 1, 0:reach, :])

    def with_ones(values):
        return jnp.concatenate([values, jnp.ones_like(values)], axis=1)

    def update(slot, query, top, total, summed):
        keys = kv[slot, 0]
        values = with_ones(kv[slot, 1])
        for r in range(ROWS // TILE):
            mine = slice(r * TILE, (r + 1) * TILE)
            score = dot_nt(query[mine, :], keys) * SCALE
            before = top[mine, :]
            peak = jnp.maximum(before, jnp.max(score, axis=1, keepdims=True))
            prob = jnp.exp2(score - jnp.concatenate([peak] * (ROWS // E), axis=1))
            fade = jnp.exp2(before - peak)
            top[mine, :] = peak
            added = dot_nn(prob.astype(jnp.bfloat16), values)
            total[mine, :] = total[mine, :] * fade + added[:, E:]
            summed[mine, :] = summed[mine, :] * fade + added[:, 0:E]

    def weigh(slot, u):
        keys = kv[slot, 0]
        for r in range(ROWS // TILE):
            mine = slice(r * TILE, (r + 1) * TILE)
            score = dot_nt(sq[mine, :], keys) * SCALE
            before = top[mine, :]
            peak = jnp.maximum(before, jnp.max(score, axis=1, keepdims=True))
            prob = jnp.exp2(score - jnp.concatenate([peak] * (ROWS // E), axis=1))
            fade = jnp.exp2(before - peak)
            top[mine, :] = peak
            weights[u, mine, :] = prob.astype(jnp.bfloat16)
            fades[u, mine, :] = fade

    def gather(slot, u):
        values = with_ones(kv[slot, 1])
        for r in range(ROWS // TILE):
            mine = slice(r * TILE, (r + 1) * TILE)
            added = dot_nn(weights[u, mine, :], values)
            summed[mine, :] = summed[mine, :] * fades[u, mine, :] + added[:, 0:E]
            total[mine, :] = total[mine, :] * fades[u, mine, :] + added[:, E:]

    @pl.when(c == 1)
    def _():
        for t in range(2):
            sib_copy(kv.at[me - 1, t], k, t).wait_recv()
        update(me - 1, sq, top, total, summed)

    def sends_up(b):
        return (k < FIRST_HELPED - 1) | ((k < CHIPS - 1) & (b > HELPER))

    def arrive(b, t):
        up_copy(kv.at[2 * b + c, t], b, t).wait_recv()

        @pl.when(sends_up(b))
        def _():
            up_copy(kv.at[2 * b + c, t], b, t).start()

        sib_copy(kv.at[2 * b + c, t], b, t).start()

    @pl.when(k == 1)
    def _():
        pass_carry()

    def step(s, _):
        b = k - s
        arrive(b, 0)
        weigh(2 * b + c, 0)
        sib_copy(kv.at[2 * b + 1 - c, 0], b, 0).wait_recv()
        weigh(2 * b + 1 - c, 1)
        arrive(b, 1)

        @pl.when((k > 1) & (b == 1))
        def _():
            pass_carry()

        gather(2 * b + c, 0)
        sib_copy(kv.at[2 * b + 1 - c, 1], b, 1).wait_recv()
        gather(2 * b + 1 - c, 1)
        return 0

    lax.fori_loop(1, jnp.where(helped, k - HELPER, k + 1), step, 0)

    @pl.when(helped)
    def _():
        pass_carry()

    tiles = [slice(r * TILE, (r + 1) * TILE) for r in range(ROWS // TILE)]

    @pl.when(k == HELPER)
    def _():
        for t in range(2):
            @pl.when(c == 0)
            def _(t=t):
                sib_copy(kv.at[me + 1, t], k, t).wait_recv()

        def one(i, _):
            j = HELPED - 1 - i
            query_copy(j).wait_recv()
            far_top[...] = jnp.full((ROWS, E), NEG, jnp.float32)
            far_total[...] = jnp.zeros((ROWS, E), jnp.float32)
            far_summed[...] = jnp.zeros((ROWS, E), jnp.float32)

            def over(u, _):
                update(2 * HELPER + 1 - u, far_query.at[j], far_top, far_total, far_summed)
                return 0

            lax.fori_loop(0, 2 * HELPER + 2, over, 0)
            stats = []
            for mine in tiles:
                far_out[j, mine, :] = (far_summed[mine, :] / far_total[mine, :]).astype(jnp.bfloat16)
                level = far_top[mine, :] + jnp.log2(far_total[mine, :])
                stats.append(jnp.transpose(level)[0:1, :])
            level = jnp.concatenate(stats, axis=0)
            high = level.astype(jnp.bfloat16).astype(jnp.float32)
            middle = (level - high).astype(jnp.bfloat16).astype(jnp.float32)
            low = level - high - middle
            far_out[j, ROWS:ROWS + STAT, :] = jnp.concatenate(
                [high, middle, low, jnp.zeros_like(low)], axis=0
            ).astype(jnp.bfloat16)
            out_copy(j).start()
            return 0

        lax.fori_loop(0, HELPED, one, 0)

    @pl.when(helped)
    def _():
        out_copy(0).wait_recv()
        parts = near_out[ROWS:ROWS + STAT, :].astype(jnp.float32)
        level = parts[0:4] + parts[4:8] + parts[8:12]
        for r, mine in enumerate(tiles):
            arrived = jnp.transpose(jnp.broadcast_to(level[r:r + 1, :], (TILE, E)))
            before = top[mine, :]
            peak = jnp.maximum(before, arrived)
            fade = jnp.exp2(before - peak)
            share = jnp.exp2(arrived - peak)
            total[mine, :] = total[mine, :] * fade + share
            summed[mine, :] = summed[mine, :] * fade + near_out[mine, :].astype(jnp.float32) * share

    for r in range(ROWS // TILE):
        mine = slice(r * TILE, (r + 1) * TILE)
        soft_out[mine, :] = (summed[mine, :] / total[mine, :]).astype(soft_out.dtype)

    @pl.when(k > 0)
    def _():
        side_carry().wait_recv()

    even = jnp.where(c == 0, 1.0, 0.0)
    odd = 1.0 - even
    f_sib = sib_state[E:E + 1, :]
    entering = (
        carry[...] * (even + odd * f_sib) + odd * sib_state[0:E, :]
    ).astype(jnp.bfloat16)
    for r in range(ROWS // TILE):
        mine = slice(r * TILE, (r + 1) * TILE)
        raw = intra[mine, :] + dot_nn(lq[mine, :], entering) * jnp.exp(cumcol[mine, :])
        mean = jnp.mean(raw * raw, axis=1, keepdims=True)
        lin_out[mine, :] = (raw * lax.rsqrt(mean + 1e-06)).astype(lin_out.dtype)

    exchange.wait_send()

    @pl.when(k < CHIPS - 1)
    def _():
        up_carry().wait_send()

    @pl.when(k > 0)
    def _():
        side_carry().wait_send()

    def drain(b, _):
        for t in range(2):
            @pl.when(sends_up(b))
            def _(t=t):
                up_copy(kv.at[2 * b + c, t], b, t).wait_send()

            @pl.when((b < k) | own_to_sib)
            def _(t=t):
                sib_copy(kv.at[2 * b + c, t], b, t).wait_send()
        return 0

    lax.fori_loop(jnp.where(helped, HELPER + 1, 0), k + 1, drain, 0)

    @pl.when(helped)
    def _():
        query_copy(0).wait_send()

    @pl.when(k == HELPER)
    def _():
        for j in range(HELPED):
            out_copy(j).wait_send()


def on_device(lin_query, lin_key, lin_value, log_decay, soft_query, soft_key, soft_value):
    def stay(array):
        return pltpu.with_memory_space_constraint(array, pltpu.MemorySpace.HBM)

    def flat(array):
        return stay(array.reshape(ROWS, E))

    vmem = pl.BlockSpec(memory_space=pltpu.VMEM)
    hbm = pl.BlockSpec(memory_space=pltpu.MemorySpace.HBM)
    f32, bf16 = jnp.float32, jnp.bfloat16
    dma = pltpu.SemaphoreType.DMA
    lin, soft = pl.pallas_call(
        kernel,
        out_shape=[jax.ShapeDtypeStruct((ROWS, E), bf16)] * 2,
        in_specs=[hbm] * 7,
        out_specs=[vmem] * 2,
        scratch_shapes=[
            pltpu.VMEM((ROWS, E), bf16),
            pltpu.VMEM((ROWS, E), bf16),
            pltpu.VMEM((ROWS, E), bf16),
            pltpu.VMEM((1, ROWS), f32),
            pltpu.VMEM((ROWS, E), bf16),
            pltpu.VMEM((2 * CHIPS, 2, ROWS, E), bf16),
            pltpu.VMEM((HELPED, ROWS, E), bf16),
            pltpu.VMEM((HELPED, ROWS + STAT, E), bf16),
            pltpu.VMEM((ROWS + STAT, E), bf16),
            pltpu.VMEM((ROWS, E), f32),
            pltpu.VMEM((ROWS, E), f32),
            pltpu.VMEM((ROWS, E), f32),
            pltpu.VMEM((2, ROWS, ROWS), bf16),
            pltpu.VMEM((2, ROWS, E), f32),
            pltpu.VMEM((ROWS, E), f32),
            pltpu.VMEM((ROWS, E), f32),
            pltpu.VMEM((ROWS, E), f32),
            pltpu.VMEM((ROWS, E), f32),
            pltpu.VMEM((ROWS, E), f32),
            pltpu.VMEM((E + 8, E), f32),
            pltpu.VMEM((E + 8, E), f32),
            pltpu.VMEM((E, E), f32),
            pltpu.VMEM((E // 2, E), f32),
            dma((7,)),
            dma((CHIPS, 2)),
            dma((CHIPS, 2)),
            dma((CHIPS, 2)),
            dma((CHIPS, 2)),
            dma,
            dma((HELPED,)),
            dma((HELPED,)),
            dma,
            dma,
            dma,
            dma((2,)),
            dma((2,)),
        ],
        compiler_params=pltpu.CompilerParams(
            collective_id=0, has_side_effects=True, vmem_limit_bytes=24 << 20
        ),
        name="hybrid_heads",
    )(
        flat(lin_query), flat(lin_key), flat(lin_value), stay(log_decay),
        flat(soft_query), flat(soft_key), flat(soft_value),
    )
    return lin.reshape(ROWS, 1, E), soft.reshape(ROWS, 1, E)


def solution(mesh):
    wide = P("ctx", "tp", None)
    return jax.shard_map(
        on_device,
        mesh=mesh,
        in_specs=(wide, wide, wide, P("tp", "ctx"), wide, wide, wide),
        out_specs=(wide, wide),
        check_vma=False,
    )
```

```python
import functools
import math

import jax
import jax.numpy as jnp
from jax import lax
from jax.experimental import pallas as pl
from jax.experimental.pallas import tpu as pltpu
from jax.sharding import PartitionSpec as P

MESH = pl.DeviceIdType.MESH
ROWS = 512
E = 128
CHIPS = 8
TILE = 128
HELPER = 1
FIRST_HELPED = 5
HELPED = CHIPS - FIRST_HELPED
STAT = 16
SCALE = math.log2(math.e) / math.sqrt(E)
NEG = -1e30


def dot_nt(a, b):
    return lax.dot_general(a, b, (((1,), (1,)), ((), ())), preferred_element_type=jnp.float32)


def dot_tn(a, b):
    return lax.dot_general(a, b, (((0,), (0,)), ((), ())), preferred_element_type=jnp.float32)


def dot_nn(a, b):
    return jnp.dot(a, b, preferred_element_type=jnp.float32)


def kernel(
    lq_hbm, lk_hbm, lv_hbm, ld_hbm, sq_hbm, sk, sv,
    lin_out, soft_out,
    lq, lk, lv, ld, sq,
    kv, far_query, far_out, near_out, far_top, far_total, far_summed,
    weights, fades, top, total, summed, intra, cumcol, state, sib_state, carry, onward,
    own_sem, up_send, z_recv, sib_send, sib_recv, q_send, q_recv, o_send, o_recv, x_send, x_recv,
    c_send, c_recv, ready,
):
    me = lax.axis_index("ctx")
    late = lax.axis_index("tp") == 0
    k = me // 2
    c = me % 2
    sib = me + 1 - 2 * c

    helped = k >= FIRST_HELPED

    def to(ctx):
        return {"ctx": ctx}

    barrier = pltpu.get_barrier_semaphore()

    def greet(device):
        pl.semaphore_signal(barrier, inc=1, device_id=device, device_id_type=MESH)

    @pl.when(jnp.logical_not(late & (me == 0)))
    def _():
        greet(to(sib))

    @pl.when(k > 0)
    def _():
        greet(to(me - 2))

    @pl.when(k == HELPER)
    def _():
        for j in range(HELPED):
            greet(to(2 * (FIRST_HELPED + j) + c))

    local = [
        pltpu.make_async_copy(src, dst, own_sem.at[i])
        for i, (src, dst) in enumerate((
            (ld_hbm, ld), (lk_hbm, lk), (lv_hbm, lv), (lq_hbm, lq), (sq_hbm, sq),
            (sk, kv.at[me, 0]), (sv, kv.at[me, 1]),
        ))
    ]
    for copy in local:
        copy.start()

    expected = jnp.where(late & (me == 1), 0, 1) + jnp.where(k < CHIPS - 1, 1, 0) + jnp.where(helped, 1, 0)
    pl.semaphore_wait(barrier, expected)

    @pl.when(late & (me == 0))
    def _():
        pl.semaphore_signal(ready, inc=1, device_id=to(sib), device_id_type=MESH)


    def remote(src, dst, send, recv, device):
        return pltpu.make_async_remote_copy(
            src_ref=src, dst_ref=dst, send_sem=send, recv_sem=recv,
            device_id=device, device_id_type=MESH,
        )

    def up_copy(src, b, t):
        return remote(src, kv.at[2 * b + c, t], up_send.at[b, t], z_recv.at[b, t], to(me + 2))

    def sib_copy(src, b, t):
        return remote(src, kv.at[2 * b + c, t], sib_send.at[b, t], sib_recv.at[b, t], to(sib))

    def query_copy(j):
        return remote(sq_hbm, far_query.at[j], q_send, q_recv.at[j], to(2 * HELPER + c))

    def out_copy(j):
        return remote(
            far_out.at[j], near_out, o_send.at[j], o_recv, to(2 * (FIRST_HELPED + j) + c)
        )

    own = (sk, sv)

    own_to_sib = (c == 0) | (k == HELPER)

    def send_own(t):
        @pl.when(k < CHIPS - 1)
        def _():
            up_copy(own[t], k, t).start()

        @pl.when(own_to_sib)
        def _():
            sib_copy(own[t], k, t).start()

    send_own(0)

    @pl.when(helped)
    def _():
        query_copy(k - FIRST_HELPED).start()

    for copy in local[:3]:
        copy.wait()

    cum = jnp.broadcast_to(ld[...], (8, ROWS))
    lane = lax.broadcasted_iota(jnp.int32, (8, ROWS), 1)
    shift = 1
    while shift < ROWS:
        cum = cum + jnp.where(lane >= shift, pltpu.roll(cum, shift, 1), 0.0)
        shift *= 2
    row = cum[0:1]
    cumcol[...] = jnp.transpose(jnp.broadcast_to(row, (E, ROWS)))
    last = cumcol[ROWS - 1:ROWS, :]
    decayed = (lk[...].astype(jnp.float32) * jnp.exp(last - cumcol[...])).astype(jnp.bfloat16)
    state[0:E, :] = dot_tn(decayed, lv[...])
    state[E:E + 8, :] = jnp.broadcast_to(jnp.exp(last), (8, E))
    exchange = remote(state, sib_state, x_send, x_recv, to(sib))

    @pl.when(late & (me == 1))
    def _():
        send_own(1)
        pl.semaphore_wait(ready, 1)

    exchange.start()

    @pl.when(k > 0)
    def _():
        send_own(1)

    half = E // 2

    def up_carry():
        return remote(
            onward, carry.at[pl.ds(c * half, half)], c_send.at[0], c_recv.at[0], to(me + 2)
        )

    def side_carry():
        return remote(
            carry.at[pl.ds(c * half, half)], carry.at[pl.ds(c * half, half)],
            c_send.at[1], c_recv.at[1], to(sib),
        )

    def chip_state():
        even = jnp.where(c == 0, 1.0, 0.0)
        odd = 1.0 - even
        f_me = state[E:E + 1, :]
        f_sib = sib_state[E:E + 1, :]
        mine = state[pl.ds(c * half, half), :]
        theirs = sib_state[pl.ds(c * half, half), :]
        f_odd = f_me * odd + f_sib * even
        s_even = mine * even + theirs * odd
        s_odd = mine * odd + theirs * even
        return f_me * f_sib, f_odd * s_even + s_odd

    exchange.wait_recv()

    @pl.when(k == 0)
    def _():
        carry[...] = jnp.zeros((E, E), jnp.float32)
        onward[...] = chip_state()[1]
        up_carry().start()

    def pass_carry():
        up_carry().wait_recv()
        side_carry().start()

        @pl.when(k < CHIPS - 1)
        def _():
            factor, added = chip_state()
            onward[...] = factor * carry[pl.ds(c * half, half), :] + added
            up_carry().start()

    @pl.when((k == 0) & jnp.logical_not(late & (me == 1)))
    def _():
        send_own(1)

    for copy in local[3:]:
        copy.wait()

    lower = (
        lax.broadcasted_iota(jnp.int32, (TILE, TILE), 0)
        >= lax.broadcasted_iota(jnp.int32, (TILE, TILE), 1)
    )
    for r in range(ROWS // TILE):
        mine = slice(r * TILE, (r + 1) * TILE)
        part = jnp.zeros((TILE, E), jnp.float32)
        for s in range(r + 1):
            theirs = slice(s * TILE, (s + 1) * TILE)
            diff = cumcol[mine, :] - row[:, theirs]
            if s == r:
                diff = jnp.where(lower, diff, NEG)
            weight = (dot_nt(lq[mine, :], lk[theirs, :]) * jnp.exp(diff)).astype(jnp.bfloat16)
            part = part + dot_nn(weight, lv[theirs, :])
        intra[mine, :] = part

    for r in range(ROWS // TILE):
        mine = slice(r * TILE, (r + 1) * TILE)
        reach = (r + 1) * TILE
        score = dot_nt(sq[mine, :], kv[me, 0, 0:reach, :]) * SCALE
        allowed = (
            lax.broadcasted_iota(jnp.int32, (TILE, reach), 0) + r * TILE
            >= lax.broadcasted_iota(jnp.int32, (TILE, reach), 1)
        )
        score = jnp.where(allowed, score, NEG)
        peak = jnp.broadcast_to(jnp.max(score, axis=1, keepdims=True), (TILE, E))
        prob = jnp.exp2(score - jnp.concatenate([peak] * (r + 1), axis=1))
        top[mine, :] = peak
        total[mine, :] = jnp.broadcast_to(jnp.sum(prob, axis=1, keepdims=True), (TILE, E))
        summed[mine, :] = dot_nn(prob.astype(jnp.bfloat16), kv[me, 1, 0:reach, :])

    def with_ones(values):
        return jnp.concatenate([values, jnp.ones_like(values)], axis=1)

    def update(slot, query, top, total, summed):
        keys = kv[slot, 0]
        values = with_ones(kv[slot, 1])
        for r in range(ROWS // TILE):
            mine = slice(r * TILE, (r + 1) * TILE)
            score = dot_nt(query[mine, :], keys) * SCALE
            before = top[mine, :]
            peak = jnp.maximum(before, jnp.max(score, axis=1, keepdims=True))
            prob = jnp.exp2(score - jnp.concatenate([peak] * (ROWS // E), axis=1))
            fade = jnp.exp2(before - peak)
            top[mine, :] = peak
            added = dot_nn(prob.astype(jnp.bfloat16), values)
            total[mine, :] = total[mine, :] * fade + added[:, E:]
            summed[mine, :] = summed[mine, :] * fade + added[:, 0:E]

    def weigh(slot, u):
        keys = kv[slot, 0]
        for r in range(ROWS // TILE):
            mine = slice(r * TILE, (r + 1) * TILE)
            score = dot_nt(sq[mine, :], keys) * SCALE
            before = top[mine, :]
            peak = jnp.maximum(before, jnp.max(score, axis=1, keepdims=True))
            prob = jnp.exp2(score - jnp.concatenate([peak] * (ROWS // E), axis=1))
            fade = jnp.exp2(before - peak)
            top[mine, :] = peak
            weights[u, mine, :] = prob.astype(jnp.bfloat16)
            fades[u, mine, :] = fade

    def gather(slot, u):
        values = with_ones(kv[slot, 1])
        for r in range(ROWS // TILE):
            mine = slice(r * TILE, (r + 1) * TILE)
            added = dot_nn(weights[u, mine, :], values)
            summed[mine, :] = summed[mine, :] * fades[u, mine, :] + added[:, 0:E]
            total[mine, :] = total[mine, :] * fades[u, mine, :] + added[:, E:]

    @pl.when(c == 1)
    def _():
        for t in range(2):
            sib_copy(kv.at[me - 1, t], k, t).wait_recv()
        update(me - 1, sq, top, total, summed)

    def sends_up(b):
        return (k < FIRST_HELPED - 1) | ((k < CHIPS - 1) & (b > HELPER))

    def arrive(b, t):
        up_copy(kv.at[2 * b + c, t], b, t).wait_recv()

        @pl.when(sends_up(b))
        def _():
            up_copy(kv.at[2 * b + c, t], b, t).start()

        sib_copy(kv.at[2 * b + c, t], b, t).start()

    @pl.when((k == 1) & jnp.logical_not(late))
    def _():
        pass_carry()

    def step(s, _):
        b = k - s
        arrive(b, 0)
        weigh(2 * b + c, 0)
        early = late & (b == 0)

        @pl.when(early)
        def _():
            arrive(b, 1)

        sib_copy(kv.at[2 * b + 1 - c, 0], b, 0).wait_recv()
        weigh(2 * b + 1 - c, 1)

        @pl.when(jnp.logical_not(early))
        def _():
            arrive(b, 1)

        @pl.when(early | ((k > 1) & (b == 1) & jnp.logical_not(late)))
        def _():
            pass_carry()

        gather(2 * b + c, 0)
        sib_copy(kv.at[2 * b + 1 - c, 1], b, 1).wait_recv()
        gather(2 * b + 1 - c, 1)
        return 0

    lax.fori_loop(1, jnp.where(helped, k - HELPER, k + 1), step, 0)

    @pl.when(helped)
    def _():
        pass_carry()

    tiles = [slice(r * TILE, (r + 1) * TILE) for r in range(ROWS // TILE)]

    @pl.when(k == HELPER)
    def _():
        for t in range(2):
            @pl.when(c == 0)
            def _(t=t):
                sib_copy(kv.at[me + 1, t], k, t).wait_recv()

        def one(i, _):
            j = HELPED - 1 - i
            query_copy(j).wait_recv()
            far_top[...] = jnp.full((ROWS, E), NEG, jnp.float32)
            far_total[...] = jnp.zeros((ROWS, E), jnp.float32)
            far_summed[...] = jnp.zeros((ROWS, E), jnp.float32)

            def over(u, _):
                update(2 * HELPER + 1 - u, far_query.at[j], far_top, far_total, far_summed)
                return 0

            lax.fori_loop(0, 2 * HELPER + 2, over, 0)
            stats = []
            for mine in tiles:
                far_out[j, mine, :] = (far_summed[mine, :] / far_total[mine, :]).astype(jnp.bfloat16)
                level = far_top[mine, :] + jnp.log2(far_total[mine, :])
                stats.append(jnp.transpose(level)[0:1, :])
            level = jnp.concatenate(stats, axis=0)
            high = level.astype(jnp.bfloat16).astype(jnp.float32)
            middle = (level - high).astype(jnp.bfloat16).astype(jnp.float32)
            low = level - high - middle
            far_out[j, ROWS:ROWS + STAT, :] = jnp.concatenate(
                [high, middle, low, jnp.zeros_like(low)], axis=0
            ).astype(jnp.bfloat16)
            out_copy(j).start()
            return 0

        lax.fori_loop(0, HELPED, one, 0)

    @pl.when(helped)
    def _():
        out_copy(0).wait_recv()
        parts = near_out[ROWS:ROWS + STAT, :].astype(jnp.float32)
        level = parts[0:4] + parts[4:8] + parts[8:12]
        for r, mine in enumerate(tiles):
            arrived = jnp.transpose(jnp.broadcast_to(level[r:r + 1, :], (TILE, E)))
            before = top[mine, :]
            peak = jnp.maximum(before, arrived)
            fade = jnp.exp2(before - peak)
            share = jnp.exp2(arrived - peak)
            total[mine, :] = total[mine, :] * fade + share
            summed[mine, :] = summed[mine, :] * fade + near_out[mine, :].astype(jnp.float32) * share

    for r in range(ROWS // TILE):
        mine = slice(r * TILE, (r + 1) * TILE)
        soft_out[mine, :] = (summed[mine, :] / total[mine, :]).astype(soft_out.dtype)

    @pl.when(k > 0)
    def _():
        side_carry().wait_recv()

    even = jnp.where(c == 0, 1.0, 0.0)
    odd = 1.0 - even
    f_sib = sib_state[E:E + 1, :]
    entering = (
        carry[...] * (even + odd * f_sib) + odd * sib_state[0:E, :]
    ).astype(jnp.bfloat16)
    for r in range(ROWS // TILE):
        mine = slice(r * TILE, (r + 1) * TILE)
        raw = intra[mine, :] + dot_nn(lq[mine, :], entering) * jnp.exp(cumcol[mine, :])
        mean = jnp.mean(raw * raw, axis=1, keepdims=True)
        lin_out[mine, :] = (raw * lax.rsqrt(mean + 1e-06)).astype(lin_out.dtype)

    exchange.wait_send()

    @pl.when(k < CHIPS - 1)
    def _():
        up_carry().wait_send()

    @pl.when(k > 0)
    def _():
        side_carry().wait_send()

    def drain(b, _):
        for t in range(2):
            @pl.when(sends_up(b))
            def _(t=t):
                up_copy(kv.at[2 * b + c, t], b, t).wait_send()

            @pl.when((b < k) | own_to_sib)
            def _(t=t):
                sib_copy(kv.at[2 * b + c, t], b, t).wait_send()
        return 0

    lax.fori_loop(jnp.where(helped, HELPER + 1, 0), k + 1, drain, 0)

    @pl.when(helped)
    def _():
        query_copy(0).wait_send()

    @pl.when(k == HELPER)
    def _():
        for j in range(HELPED):
            out_copy(j).wait_send()


def on_device(lin_query, lin_key, lin_value, log_decay, soft_query, soft_key, soft_value):
    def stay(array):
        return pltpu.with_memory_space_constraint(array, pltpu.MemorySpace.HBM)

    def flat(array):
        return stay(array.reshape(ROWS, E))

    vmem = pl.BlockSpec(memory_space=pltpu.VMEM)
    hbm = pl.BlockSpec(memory_space=pltpu.MemorySpace.HBM)
    f32, bf16 = jnp.float32, jnp.bfloat16
    dma = pltpu.SemaphoreType.DMA
    lin, soft = pl.pallas_call(
        kernel,
        out_shape=[jax.ShapeDtypeStruct((ROWS, E), bf16)] * 2,
        in_specs=[hbm] * 7,
        out_specs=[vmem] * 2,
        scratch_shapes=[
            pltpu.VMEM((ROWS, E), bf16),
            pltpu.VMEM((ROWS, E), bf16),
            pltpu.VMEM((ROWS, E), bf16),
            pltpu.VMEM((1, ROWS), f32),
            pltpu.VMEM((ROWS, E), bf16),
            pltpu.VMEM((2 * CHIPS, 2, ROWS, E), bf16),
            pltpu.VMEM((HELPED, ROWS, E), bf16),
            pltpu.VMEM((HELPED, ROWS + STAT, E), bf16),
            pltpu.VMEM((ROWS + STAT, E), bf16),
            pltpu.VMEM((ROWS, E), f32),
            pltpu.VMEM((ROWS, E), f32),
            pltpu.VMEM((ROWS, E), f32),
            pltpu.VMEM((2, ROWS, ROWS), bf16),
            pltpu.VMEM((2, ROWS, E), f32),
            pltpu.VMEM((ROWS, E), f32),
            pltpu.VMEM((ROWS, E), f32),
            pltpu.VMEM((ROWS, E), f32),
            pltpu.VMEM((ROWS, E), f32),
            pltpu.VMEM((ROWS, E), f32),
            pltpu.VMEM((E + 8, E), f32),
            pltpu.VMEM((E + 8, E), f32),
            pltpu.VMEM((E, E), f32),
            pltpu.VMEM((E // 2, E), f32),
            dma((7,)),
            dma((CHIPS, 2)),
            dma((CHIPS, 2)),
            dma((CHIPS, 2)),
            dma((CHIPS, 2)),
            dma,
            dma((HELPED,)),
            dma((HELPED,)),
            dma,
            dma,
            dma,
            dma((2,)),
            dma((2,)),
            pltpu.SemaphoreType.REGULAR,
        ],
        compiler_params=pltpu.CompilerParams(
            collective_id=0, has_side_effects=True, vmem_limit_bytes=24 << 20
        ),
        name="hybrid_heads",
    )(
        flat(lin_query), flat(lin_key), flat(lin_value), stay(log_decay),
        flat(soft_query), flat(soft_key), flat(soft_value),
    )
    return lin.reshape(ROWS, 1, E), soft.reshape(ROWS, 1, E)


def solution(mesh):
    wide = P("ctx", "tp", None)
    return jax.shard_map(
        on_device,
        mesh=mesh,
        in_specs=(wide, wide, wide, P("tp", "ctx"), wide, wide, wide),
        out_specs=(wide, wide),
        check_vma=False,
    )
```

```python
import functools
import math

import jax
import jax.numpy as jnp
from jax import lax
from jax.experimental import pallas as pl
from jax.experimental.pallas import tpu as pltpu
from jax.sharding import PartitionSpec as P

MESH = pl.DeviceIdType.MESH
ROWS = 512
E = 128
CHIPS = 8
TILE = 128
HELPER = 1
FIRST_HELPED = 5
HELPED = CHIPS - FIRST_HELPED
STAT = 16
SCALE = math.log2(math.e) / math.sqrt(E)
NEG = -1e30


def dot_nt(a, b):
    return lax.dot_general(a, b, (((1,), (1,)), ((), ())), preferred_element_type=jnp.float32)


def dot_tn(a, b):
    return lax.dot_general(a, b, (((0,), (0,)), ((), ())), preferred_element_type=jnp.float32)


def dot_nn(a, b):
    return jnp.dot(a, b, preferred_element_type=jnp.float32)


def kernel(
    lq_hbm, lk_hbm, lv_hbm, ld_hbm, sq_hbm, sk, sv,
    lin_out, soft_out,
    lq, lk, lv, ld, sq,
    kv, far_query, far_out, near_out, far_top, far_total, far_summed,
    weights, fades, top, total, summed, intra, cumcol, state, sib_state, carry, onward,
    own_sem, up_send, z_recv, sib_send, sib_recv, q_send, q_recv, o_send, o_recv, x_send, x_recv,
    c_send, c_recv, ready,
):
    me = lax.axis_index("ctx")
    late = lax.axis_index("tp") == 0
    k = me // 2
    c = me % 2
    sib = me + 1 - 2 * c

    helped = k >= FIRST_HELPED

    def to(ctx):
        return {"ctx": ctx}

    barrier = pltpu.get_barrier_semaphore()

    def greet(device):
        pl.semaphore_signal(barrier, inc=1, device_id=device, device_id_type=MESH)

    @pl.when(jnp.logical_not(late & (me == 0)))
    def _():
        greet(to(sib))

    @pl.when(k > 0)
    def _():
        greet(to(me - 2))

    @pl.when(k == HELPER)
    def _():
        for j in range(HELPED):
            greet(to(2 * (FIRST_HELPED + j) + c))

    local = [
        pltpu.make_async_copy(src, dst, own_sem.at[i])
        for i, (src, dst) in enumerate((
            (ld_hbm, ld), (lk_hbm, lk), (lv_hbm, lv), (lq_hbm, lq), (sq_hbm, sq),
            (sk, kv.at[me, 0]), (sv, kv.at[me, 1]),
        ))
    ]
    for copy in local:
        copy.start()

    expected = jnp.where(late & (me == 1), 0, 1) + jnp.where(k < CHIPS - 1, 1, 0) + jnp.where(helped, 1, 0)
    pl.semaphore_wait(barrier, expected)

    @pl.when(late & (me == 0))
    def _():
        pl.semaphore_signal(ready, inc=1, device_id=to(sib), device_id_type=MESH)


    def remote(src, dst, send, recv, device):
        return pltpu.make_async_remote_copy(
            src_ref=src, dst_ref=dst, send_sem=send, recv_sem=recv,
            device_id=device, device_id_type=MESH,
        )

    def up_copy(src, b, t):
        return remote(src, kv.at[2 * b + c, t], up_send.at[b, t], z_recv.at[b, t], to(me + 2))

    def sib_copy(src, b, t):
        return remote(src, kv.at[2 * b + c, t], sib_send.at[b, t], sib_recv.at[b, t], to(sib))

    def query_copy(j):
        return remote(sq_hbm, far_query.at[j], q_send, q_recv.at[j], to(2 * HELPER + c))

    def out_copy(j):
        return remote(
            far_out.at[j], near_out, o_send.at[j], o_recv, to(2 * (FIRST_HELPED + j) + c)
        )

    own = (sk, sv)

    own_to_sib = (c == 0) | (k == HELPER)

    def send_own(t):
        @pl.when(k < CHIPS - 1)
        def _():
            up_copy(own[t], k, t).start()

        @pl.when(own_to_sib)
        def _():
            sib_copy(own[t], k, t).start()

    send_own(0)

    @pl.when(helped)
    def _():
        query_copy(k - FIRST_HELPED).start()

    for copy in local[:3]:
        copy.wait()

    cum = jnp.broadcast_to(ld[...], (8, ROWS))
    lane = lax.broadcasted_iota(jnp.int32, (8, ROWS), 1)
    shift = 1
    while shift < ROWS:
        cum = cum + jnp.where(lane >= shift, pltpu.roll(cum, shift, 1), 0.0)
        shift *= 2
    row = cum[0:1]
    cumcol[...] = jnp.transpose(jnp.broadcast_to(row, (E, ROWS)))
    last = cumcol[ROWS - 1:ROWS, :]
    decayed = (lk[...].astype(jnp.float32) * jnp.exp(last - cumcol[...])).astype(jnp.bfloat16)
    state[0:E, :] = dot_tn(decayed, lv[...])
    state[E:E + 8, :] = jnp.broadcast_to(jnp.exp(last), (8, E))
    exchange = remote(state, sib_state, x_send, x_recv, to(sib))

    @pl.when(late & (me == 1))
    def _():
        send_own(1)
        pl.semaphore_wait(ready, 1)

    exchange.start()

    @pl.when(k > 0)
    def _():
        send_own(1)

    half = E // 2

    def up_carry():
        return remote(
            onward, carry.at[pl.ds(c * half, half)], c_send.at[0], c_recv.at[0], to(me + 2)
        )

    def side_carry():
        return remote(
            carry.at[pl.ds(c * half, half)], carry.at[pl.ds(c * half, half)],
            c_send.at[1], c_recv.at[1], to(sib),
        )

    def chip_state():
        even = jnp.where(c == 0, 1.0, 0.0)
        odd = 1.0 - even
        f_me = state[E:E + 1, :]
        f_sib = sib_state[E:E + 1, :]
        mine = state[pl.ds(c * half, half), :]
        theirs = sib_state[pl.ds(c * half, half), :]
        f_odd = f_me * odd + f_sib * even
        s_even = mine * even + theirs * odd
        s_odd = mine * odd + theirs * even
        return f_me * f_sib, f_odd * s_even + s_odd

    exchange.wait_recv()

    @pl.when(k == 0)
    def _():
        carry[...] = jnp.zeros((E, E), jnp.float32)
        onward[...] = chip_state()[1]
        up_carry().start()

    def pass_carry():
        up_carry().wait_recv()
        side_carry().start()

        @pl.when(k < CHIPS - 1)
        def _():
            factor, added = chip_state()
            onward[...] = factor * carry[pl.ds(c * half, half), :] + added
            up_carry().start()

    @pl.when((k == 0) & jnp.logical_not(late & (me == 1)))
    def _():
        send_own(1)

    for copy in local[3:]:
        copy.wait()

    lower = (
        lax.broadcasted_iota(jnp.int32, (TILE, TILE), 0)
        >= lax.broadcasted_iota(jnp.int32, (TILE, TILE), 1)
    )
    for r in range(ROWS // TILE):
        mine = slice(r * TILE, (r + 1) * TILE)
        part = jnp.zeros((TILE, E), jnp.float32)
        for s in range(r + 1):
            theirs = slice(s * TILE, (s + 1) * TILE)
            diff = cumcol[mine, :] - row[:, theirs]
            if s == r:
                diff = jnp.where(lower, diff, NEG)
            weight = (dot_nt(lq[mine, :], lk[theirs, :]) * jnp.exp(diff)).astype(jnp.bfloat16)
            part = part + dot_nn(weight, lv[theirs, :])
        intra[mine, :] = part

    for r in range(ROWS // TILE):
        mine = slice(r * TILE, (r + 1) * TILE)
        reach = (r + 1) * TILE
        score = dot_nt(sq[mine, :], kv[me, 0, 0:reach, :]) * SCALE
        allowed = (
            lax.broadcasted_iota(jnp.int32, (TILE, reach), 0) + r * TILE
            >= lax.broadcasted_iota(jnp.int32, (TILE, reach), 1)
        )
        score = jnp.where(allowed, score, NEG)
        peak = jnp.broadcast_to(jnp.max(score, axis=1, keepdims=True), (TILE, E))
        prob = jnp.exp2(score - jnp.concatenate([peak] * (r + 1), axis=1))
        top[mine, :] = peak
        total[mine, :] = jnp.broadcast_to(jnp.sum(prob, axis=1, keepdims=True), (TILE, E))
        summed[mine, :] = dot_nn(prob.astype(jnp.bfloat16), kv[me, 1, 0:reach, :])

    def with_ones(values):
        return jnp.concatenate([values, jnp.ones_like(values)], axis=1)

    def update(slot, query, top, total, summed):
        keys = kv[slot, 0]
        values = with_ones(kv[slot, 1])
        for r in range(ROWS // TILE):
            mine = slice(r * TILE, (r + 1) * TILE)
            score = dot_nt(query[mine, :], keys) * SCALE
            before = top[mine, :]
            peak = jnp.maximum(before, jnp.max(score, axis=1, keepdims=True))
            prob = jnp.exp2(score - jnp.concatenate([peak] * (ROWS // E), axis=1))
            fade = jnp.exp2(before - peak)
            top[mine, :] = peak
            added = dot_nn(prob.astype(jnp.bfloat16), values)
            total[mine, :] = total[mine, :] * fade + added[:, E:]
            summed[mine, :] = summed[mine, :] * fade + added[:, 0:E]

    def weigh(slot, u):
        keys = kv[slot, 0]
        for r in range(ROWS // TILE):
            mine = slice(r * TILE, (r + 1) * TILE)
            score = dot_nt(sq[mine, :], keys) * SCALE
            before = top[mine, :]
            peak = jnp.maximum(before, jnp.max(score, axis=1, keepdims=True))
            prob = jnp.exp2(score - jnp.concatenate([peak] * (ROWS // E), axis=1))
            fade = jnp.exp2(before - peak)
            top[mine, :] = peak
            weights[u, mine, :] = prob.astype(jnp.bfloat16)
            fades[u, mine, :] = fade

    def gather(slot, u):
        values = with_ones(kv[slot, 1])
        for r in range(ROWS // TILE):
            mine = slice(r * TILE, (r + 1) * TILE)
            added = dot_nn(weights[u, mine, :], values)
            summed[mine, :] = summed[mine, :] * fades[u, mine, :] + added[:, 0:E]
            total[mine, :] = total[mine, :] * fades[u, mine, :] + added[:, E:]

    @pl.when(c == 1)
    def _():
        for t in range(2):
            sib_copy(kv.at[me - 1, t], k, t).wait_recv()
        update(me - 1, sq, top, total, summed)

    def sends_up(b):
        return (k < FIRST_HELPED - 1) | ((k < CHIPS - 1) & (b > HELPER))

    def arrive(b, t):
        up_copy(kv.at[2 * b + c, t], b, t).wait_recv()

        @pl.when(sends_up(b))
        def _():
            up_copy(kv.at[2 * b + c, t], b, t).start()

        sib_copy(kv.at[2 * b + c, t], b, t).start()

    @pl.when((k == 1) & jnp.logical_not(late))
    def _():
        pass_carry()

    def step(s, _):
        b = k - s
        early = late & (b == 0)
        arrive(b, 0)

        @pl.when(early & (c == 1))
        def _():
            arrive(b, 1)

        @pl.when(early)
        def _():
            pass_carry()

        @pl.when(early & (c == 0))
        def _():
            arrive(b, 1)

        weigh(2 * b + c, 0)
        sib_copy(kv.at[2 * b + 1 - c, 0], b, 0).wait_recv()
        weigh(2 * b + 1 - c, 1)

        @pl.when(jnp.logical_not(early))
        def _():
            arrive(b, 1)

        @pl.when((k > 1) & (b == 1) & jnp.logical_not(late))
        def _():
            pass_carry()

        gather(2 * b + c, 0)
        sib_copy(kv.at[2 * b + 1 - c, 1], b, 1).wait_recv()
        gather(2 * b + 1 - c, 1)
        return 0

    lax.fori_loop(1, jnp.where(helped, k - HELPER, k + 1), step, 0)

    @pl.when(helped)
    def _():
        pass_carry()

    tiles = [slice(r * TILE, (r + 1) * TILE) for r in range(ROWS // TILE)]

    @pl.when(k == HELPER)
    def _():
        for t in range(2):
            @pl.when(c == 0)
            def _(t=t):
                sib_copy(kv.at[me + 1, t], k, t).wait_recv()

        def one(i, _):
            j = HELPED - 1 - i
            query_copy(j).wait_recv()
            far_top[...] = jnp.full((ROWS, E), NEG, jnp.float32)
            far_total[...] = jnp.zeros((ROWS, E), jnp.float32)
            far_summed[...] = jnp.zeros((ROWS, E), jnp.float32)

            def over(u, _):
                update(2 * HELPER + 1 - u, far_query.at[j], far_top, far_total, far_summed)
                return 0

            lax.fori_loop(0, 2 * HELPER + 2, over, 0)
            stats = []
            for mine in tiles:
                far_out[j, mine, :] = (far_summed[mine, :] / far_total[mine, :]).astype(jnp.bfloat16)
                level = far_top[mine, :] + jnp.log2(far_total[mine, :])
                stats.append(jnp.transpose(level)[0:1, :])
            level = jnp.concatenate(stats, axis=0)
            high = level.astype(jnp.bfloat16).astype(jnp.float32)
            middle = (level - high).astype(jnp.bfloat16).astype(jnp.float32)
            low = level - high - middle
            far_out[j, ROWS:ROWS + STAT, :] = jnp.concatenate(
                [high, middle, low, jnp.zeros_like(low)], axis=0
            ).astype(jnp.bfloat16)
            out_copy(j).start()
            return 0

        lax.fori_loop(0, HELPED, one, 0)

    @pl.when(helped)
    def _():
        out_copy(0).wait_recv()
        parts = near_out[ROWS:ROWS + STAT, :].astype(jnp.float32)
        level = parts[0:4] + parts[4:8] + parts[8:12]
        for r, mine in enumerate(tiles):
            arrived = jnp.transpose(jnp.broadcast_to(level[r:r + 1, :], (TILE, E)))
            before = top[mine, :]
            peak = jnp.maximum(before, arrived)
            fade = jnp.exp2(before - peak)
            share = jnp.exp2(arrived - peak)
            total[mine, :] = total[mine, :] * fade + share
            summed[mine, :] = summed[mine, :] * fade + near_out[mine, :].astype(jnp.float32) * share

    for r in range(ROWS // TILE):
        mine = slice(r * TILE, (r + 1) * TILE)
        soft_out[mine, :] = (summed[mine, :] / total[mine, :]).astype(soft_out.dtype)

    @pl.when(k > 0)
    def _():
        side_carry().wait_recv()

    even = jnp.where(c == 0, 1.0, 0.0)
    odd = 1.0 - even
    f_sib = sib_state[E:E + 1, :]
    entering = (
        carry[...] * (even + odd * f_sib) + odd * sib_state[0:E, :]
    ).astype(jnp.bfloat16)
    for r in range(ROWS // TILE):
        mine = slice(r * TILE, (r + 1) * TILE)
        raw = intra[mine, :] + dot_nn(lq[mine, :], entering) * jnp.exp(cumcol[mine, :])
        mean = jnp.mean(raw * raw, axis=1, keepdims=True)
        lin_out[mine, :] = (raw * lax.rsqrt(mean + 1e-06)).astype(lin_out.dtype)

    exchange.wait_send()

    @pl.when(k < CHIPS - 1)
    def _():
        up_carry().wait_send()

    @pl.when(k > 0)
    def _():
        side_carry().wait_send()

    def drain(b, _):
        for t in range(2):
            @pl.when(sends_up(b))
            def _(t=t):
                up_copy(kv.at[2 * b + c, t], b, t).wait_send()

            @pl.when((b < k) | own_to_sib)
            def _(t=t):
                sib_copy(kv.at[2 * b + c, t], b, t).wait_send()
        return 0

    lax.fori_loop(jnp.where(helped, HELPER + 1, 0), k + 1, drain, 0)

    @pl.when(helped)
    def _():
        query_copy(0).wait_send()

    @pl.when(k == HELPER)
    def _():
        for j in range(HELPED):
            out_copy(j).wait_send()


def on_device(lin_query, lin_key, lin_value, log_decay, soft_query, soft_key, soft_value):
    def stay(array):
        return pltpu.with_memory_space_constraint(array, pltpu.MemorySpace.HBM)

    def flat(array):
        return stay(array.reshape(ROWS, E))

    vmem = pl.BlockSpec(memory_space=pltpu.VMEM)
    hbm = pl.BlockSpec(memory_space=pltpu.MemorySpace.HBM)
    f32, bf16 = jnp.float32, jnp.bfloat16
    dma = pltpu.SemaphoreType.DMA
    lin, soft = pl.pallas_call(
        kernel,
        out_shape=[jax.ShapeDtypeStruct((ROWS, E), bf16)] * 2,
        in_specs=[hbm] * 7,
        out_specs=[vmem] * 2,
        scratch_shapes=[
            pltpu.VMEM((ROWS, E), bf16),
            pltpu.VMEM((ROWS, E), bf16),
            pltpu.VMEM((ROWS, E), bf16),
            pltpu.VMEM((1, ROWS), f32),
            pltpu.VMEM((ROWS, E), bf16),
            pltpu.VMEM((2 * CHIPS, 2, ROWS, E), bf16),
            pltpu.VMEM((HELPED, ROWS, E), bf16),
            pltpu.VMEM((HELPED, ROWS + STAT, E), bf16),
            pltpu.VMEM((ROWS + STAT, E), bf16),
            pltpu.VMEM((ROWS, E), f32),
            pltpu.VMEM((ROWS, E), f32),
            pltpu.VMEM((ROWS, E), f32),
            pltpu.VMEM((2, ROWS, ROWS), bf16),
            pltpu.VMEM((2, ROWS, E), f32),
            pltpu.VMEM((ROWS, E), f32),
            pltpu.VMEM((ROWS, E), f32),
            pltpu.VMEM((ROWS, E), f32),
            pltpu.VMEM((ROWS, E), f32),
            pltpu.VMEM((ROWS, E), f32),
            pltpu.VMEM((E + 8, E), f32),
            pltpu.VMEM((E + 8, E), f32),
            pltpu.VMEM((E, E), f32),
            pltpu.VMEM((E // 2, E), f32),
            dma((7,)),
            dma((CHIPS, 2)),
            dma((CHIPS, 2)),
            dma((CHIPS, 2)),
            dma((CHIPS, 2)),
            dma,
            dma((HELPED,)),
            dma((HELPED,)),
            dma,
            dma,
            dma,
            dma((2,)),
            dma((2,)),
            pltpu.SemaphoreType.REGULAR,
        ],
        compiler_params=pltpu.CompilerParams(
            collective_id=0, has_side_effects=True, vmem_limit_bytes=24 << 20
        ),
        name="hybrid_heads",
    )(
        flat(lin_query), flat(lin_key), flat(lin_value), stay(log_decay),
        flat(soft_query), flat(soft_key), flat(soft_value),
    )
    return lin.reshape(ROWS, 1, E), soft.reshape(ROWS, 1, E)


def solution(mesh):
    wide = P("ctx", "tp", None)
    return jax.shard_map(
        on_device,
        mesh=mesh,
        in_specs=(wide, wide, wide, P("tp", "ctx"), wide, wide, wide),
        out_specs=(wide, wide),
        check_vma=False,
    )
```
